256 devices in a mesh: section: 16 (over z, core), mp: 8 (over x, y_hi), dp: 2 (over y_lo).
Axes of the slice: x: 4, y: 4 (y_hi: 2, y_lo: 2; y = y_hi * 2 + y_lo), z: 8, core: 2. Of those that a mesh axis runs over, the one named last changes fastest.
Arguments:
- enc_out: bfloat16 [2, 512, 4096], P('dp', 'mp', 'section'), may hold values from -6 to 6
- kv_weight: bfloat16 [16, 4096, 2, 4096], P('section', None, None, 'mp'), may hold values from -0.09375 to 0.09375
- dec_query: bfloat16 [16, 2, 512, 4096], P('section', 'dp', None, 'mp'), may hold values from -120 to 120
- ctx_grad: bfloat16 [16, 2, 512, 4096], P('section', 'dp', None, 'mp'), may hold values from -6 to 6
- enc_seg: int32 [2, 512], P('dp'), may hold values from 0 to 7, never falling along the last dimension, each value on 1 to 128 neighbouring positions
- dec_seg: int32 [2, 512], P('dp'), may hold values from 0 to 7, never falling along the last dimension, each value on 1 to 128 neighbouring positions
Outputs:
- context: bfloat16 [16, 2, 512, 4096], P('section', 'dp', None, 'mp')
- enc_grad: float32 [2, 512, 4096], P('dp', 'mp', 'section')
The draws below stay inside these ranges and needn't reach their ends.
Inputs may be any that keep to these rules, and one draw needn't show every extreme that they name: `enc_seg`: document ids never fall along a sequence and every id appears. `dec_seg`: document ids never fall along a sequence and every id appears.
All inputs are finite; a program needn't handle non-finite values.
Results may differ from the reference program's by a relative error of at most 0.04.
The reference program's roundings to bfloat16 on the way (of `key_values`, `probs_low`, `grad_values`, `grad_scores` and `grad_keys`) count: a program that leaves them out, or rounds other values in their place, can miss the bound.
Values may be sent and summed in bfloat16 or wider, within the bound.
No kernel may reach another device: no remote copies, remote signals or barrier semaphores. Data moves between devices by JAX's collectives and lax.ppermute only.
A program may use at most 128 MiB of HBM per device.

```python
import math
import jax
import jax.numpy as jnp
import numpy as np
from jax import lax

D = 4096
HD = 256
HEADS = 16
DLEN = 512
SEGS = 8
LEN = 512
N_SECTION = 16
N_DP = 2


def draw_dec_query(key, part):
    shape = (N_SECTION, N_DP, DLEN, HEADS * HD)
    return jax.random.truncated_normal(key, -4.0, 4.0, shape, jnp.float32).astype(jnp.bfloat16)


def levels(rng, dims, cuts, low, largest):
    def one(dim, shards_of):
        heights = jax.random.uniform(jax.random.fold_in(jax.random.fold_in(rng, 6), dim), (shards_of,), jnp.float32, low / len(cuts), largest / len(cuts))
        return jnp.repeat(jnp.exp(heights), dims[dim] // shards_of).reshape((-1,) + (1,) * (len(dims) - dim - 1))

    gain = one(*cuts[0])
    for cut in cuts[1:]:
        gain = gain * one(*cut)
    return gain


def profile(count, total, bound, slope):
    loads = [(1 << 20) // math.isqrt(grade ** slope) + 1 for grade in range(2, count + 1)]
    spare, holding = total - bound - (count - 1), [1] * (count - 1)
    while spare > 0:
        free = [i for i in range(count - 1) if holding[i] < bound]
        mass, remaining = sum([loads[i] for i in free]), spare
        for i in free:
            more = min(bound - holding[i], max(1, remaining * loads[i] // mass), spare)
            holding[i] = holding[i] + more
            spare = spare - more
    return np.array([bound] + holding)


def ragged_sizes(rng, count, total, reach, lean):
    if count == 2:
        one = jax.random.randint(rng, (), max(1, total - reach), min(reach, total - 1) + 1)
        return jnp.stack([one, total - one])
    tallies = jnp.asarray(profile(count, total, reach, lean), jnp.int32)
    twos = (count - 1) // 2
    source_of, sink = tallies[1:1 + 2 * twos:2], tallies[2:2 + 2 * twos:2]
    margin = jnp.minimum(source_of - 1, reach - sink)
    moved = jax.random.randint(jax.random.fold_in(rng, 1), (twos,), 0, 1 << 20) % (margin + 1)
    tallies = tallies.at[1:1 + 2 * twos:2].set(source_of - moved).at[2:2 + 2 * twos:2].set(sink + moved)
    return tallies[jax.random.permutation(jax.random.fold_in(rng, 2), count)]


def normal_values(stream_key, extent, scale, reach, shards=(), held_as=jnp.bfloat16):
    entries = scale * jax.random.normal(stream_key, extent, jnp.float32)
    if shards:
        entries = entries * levels(stream_key, extent, shards, -0.22, 0.18)
    return jnp.clip(entries, -reach, reach).astype(held_as)


def setup_inputs(seed: int = 0) -> dict:
    seeds = jax.random.split(jax.random.key(seed), 7)
    return {
        "enc_out": normal_values(seeds[0], (N_DP, LEN, D), 1.0, 6.0, ((0, 2), (1, 8), (2, 16))),
        "kv_weight": normal_values(seeds[1], (N_SECTION, D, 2, HEADS * HD), D ** -0.5, 0.09375, ((0, 16), (3, 8))),
        "dec_query": draw_dec_query(jax.random.fold_in(seeds[6], 71), 0),
        "ctx_grad": normal_values(seeds[3], (N_SECTION, N_DP, DLEN, HEADS * HD), 1.0, 6.0, ((0, 16), (1, 2), (3, 8))),
        "enc_seg": jax.vmap(lambda own: jnp.searchsorted(jnp.cumsum(ragged_sizes(own, SEGS, LEN, LEN // 4, 1)), jnp.arange(LEN), side="right"))(jax.random.split(seeds[4], N_DP)).reshape((N_DP, LEN)).astype(jnp.int32),
        "dec_seg": jax.vmap(lambda own: jnp.searchsorted(jnp.cumsum(ragged_sizes(own, SEGS, DLEN, DLEN // 4, 1)), jnp.arange(DLEN), side="right"))(jax.random.split(seeds[5], N_DP)).reshape((N_DP, DLEN)).astype(jnp.int32),
    }


def attend(query, keys, values, grad, same_doc):
    scale = HD ** -0.5
    scores = jnp.einsum("qhd,khd->hqk", query.astype(jnp.float32), keys.astype(jnp.float32)) * scale
    scores = jnp.where(same_doc[None], scores, -1e30)
    top_score = jnp.max(scores, axis=-1, keepdims=True)
    raised = jnp.exp(scores - top_score)
    probs = raised / jnp.sum(raised, axis=-1, keepdims=True)
    probs_low = probs.astype(jnp.bfloat16)
    context = jnp.einsum("hqk,khd->qhd", probs_low.astype(jnp.float32), values.astype(jnp.float32)).astype(jnp.bfloat16)
    grad_values = jnp.einsum("hqk,qhd->khd", probs_low.astype(jnp.float32), grad.astype(jnp.float32)).astype(jnp.bfloat16)
    grad_probs = jnp.einsum("qhd,khd->hqk", grad.astype(jnp.float32), values.astype(jnp.float32))
    inner_sum = jnp.sum(probs * grad_probs, axis=-1, keepdims=True)
    grad_scores = (probs * (grad_probs - inner_sum) * scale).astype(jnp.bfloat16)
    grad_keys = jnp.einsum("hqk,qhd->khd", grad_scores.astype(jnp.float32), query.astype(jnp.float32)).astype(jnp.bfloat16)
    return context, grad_keys, grad_values


def reference(enc_out, kv_weight, dec_query, ctx_grad, enc_seg, dec_seg):
    width = HEADS * HD

    def one_section(carry, inputs):
        weight, query, grad = inputs
        flat_weight = weight.reshape(D, 2 * width)
        grad_terms = []
        context_list = []
        for batch in range(N_DP):
            key_values = jnp.dot(enc_out[batch], flat_weight, preferred_element_type=jnp.float32).astype(jnp.bfloat16)
            keys = key_values[:, :width].reshape(LEN, HEADS, HD)
            values = key_values[:, width:].reshape(LEN, HEADS, HD)
            same_doc = dec_seg[batch][:, None] == enc_seg[batch][None, :]
            context, grad_keys, grad_values = attend(query[batch].reshape(DLEN, HEADS, HD), keys, values, grad[batch].reshape(DLEN, HEADS, HD), same_doc)
            grad_both = jnp.concatenate([grad_keys.reshape(LEN, width), grad_values.reshape(LEN, width)], axis=1)
            grad_terms.append(lax.dot_general(grad_both, flat_weight, (((1,), (1,)), ((), ())), preferred_element_type=jnp.float32))
            context_list.append(context.reshape(DLEN, width))
        return carry + jnp.stack(grad_terms), jnp.stack(context_list)

    total, contexts = lax.scan(one_section, jnp.zeros((N_DP, LEN, D), jnp.float32), (kv_weight, dec_query, ctx_grad))
    return contexts, total
```

```python
import functools

import jax
import jax.numpy as jnp
from jax import lax
from jax.experimental import pallas as pl
from jax.experimental.pallas import tpu as pltpu
from jax.sharding import Mesh, PartitionSpec as P

HD = 256
NZ, NC, NX, NY, ND = 8, 2, 4, 2, 2
TB = 64
FB = 256
VMEM = 48 << 20


def project_kernel(core_ref, *refs):
    own, other, w_ref, out_ref, acc_ref = refs[:8], refs[8:16], refs[16], refs[17], refs[18]
    step = pl.program_id(0)
    core = core_ref[0]
    own_rows = jnp.concatenate([r[0] for r in own], axis=0)
    other_rows = jnp.concatenate([r[0] for r in other], axis=0)
    w_own = w_ref[pl.ds(pl.multiple_of(core * FB, FB), FB), :]
    w_other = w_ref[pl.ds(pl.multiple_of((1 - core) * FB, FB), FB), :]
    part = jnp.dot(own_rows, w_own, preferred_element_type=jnp.float32)
    part = part + jnp.dot(other_rows, w_other, preferred_element_type=jnp.float32)

    @pl.when(step == 0)
    def _():
        acc_ref[...] = part

    @pl.when(step > 0)
    def _():
        acc_ref[...] = acc_ref[...] + part

    @pl.when(step == NZ - 1)
    def _():
        out_ref[...] = acc_ref[...].astype(jnp.bfloat16)


def project(core, own, other, weight):
    width = weight.shape[1]
    rows = 8 * TB
    block = pl.BlockSpec((1, TB, FB), lambda z, c: (z, 0, 0))
    return pl.pallas_call(
        project_kernel,
        grid_spec=pltpu.PrefetchScalarGridSpec(
            num_scalar_prefetch=1,
            grid=(NZ,),
            in_specs=[block] * 16 + [pl.BlockSpec((2 * FB, width), lambda z, c: (z, 0))],
            out_specs=pl.BlockSpec((rows, width), lambda z, c: (0, 0)),
            scratch_shapes=[pltpu.VMEM((rows, width), jnp.float32)],
        ),
        out_shape=jax.ShapeDtypeStruct((rows, width), jnp.bfloat16),
        compiler_params=pltpu.CompilerParams(vmem_limit_bytes=VMEM),
        name="project",
    )(core, *own, *other, weight)


NT = (((1,), (1,)), ((), ()))
TN = (((0,), (0,)), ((), ()))


def attend_kernel(q_ref, g_ref, k_ref, v_ref, es_ref, ds_ref, ctx_ref, gk_ref, gv_ref):
    scale = HD ** -0.5
    q, g, k, v = q_ref[...], g_ref[...], k_ref[...], v_ref[...]
    same = es_ref[...] == ds_ref[...]
    scores = lax.dot_general(k, q, NT, preferred_element_type=jnp.float32) * scale
    scores = jnp.where(same, scores, -1e30)
    top = jnp.max(scores, axis=0, keepdims=True)
    raised = jnp.exp(scores - top)
    probs = raised / jnp.sum(raised, axis=0, keepdims=True)
    low = probs.astype(jnp.bfloat16)
    ctx_ref[...] = lax.dot_general(low, v, TN, preferred_element_type=jnp.float32).astype(jnp.bfloat16)
    gv_ref[...] = jnp.dot(low, g, preferred_element_type=jnp.float32).astype(jnp.bfloat16)
    gp = lax.dot_general(v, g, NT, preferred_element_type=jnp.float32)
    inner = jnp.sum(probs * gp, axis=0, keepdims=True)
    gs = (probs * (gp - inner) * scale).astype(jnp.bfloat16)
    gk_ref[...] = jnp.dot(gs, q, preferred_element_type=jnp.float32).astype(jnp.bfloat16)


def attend(query, grad, key_values, enc_col, dec_row):
    dec, width = query.shape
    enc = key_values.shape[0]
    heads = width // HD
    head = pl.BlockSpec((dec, HD), lambda h: (0, h))
    key = pl.BlockSpec((enc, HD), lambda h: (0, h))
    value = pl.BlockSpec((enc, HD), lambda h: (0, heads + h))
    return pl.pallas_call(
        attend_kernel,
        grid=(heads,),
        in_specs=[head, head, key, value, pl.BlockSpec((enc, 1), lambda h: (0, 0)), pl.BlockSpec((1, dec), lambda h: (0, 0))],
        out_specs=[head, key, key],
        out_shape=[
            jax.ShapeDtypeStruct((dec, width), jnp.bfloat16),
            jax.ShapeDtypeStruct((enc, width), jnp.bfloat16),
            jax.ShapeDtypeStruct((enc, width), jnp.bfloat16),
        ],
        compiler_params=pltpu.CompilerParams(vmem_limit_bytes=VMEM),
        name="attend",
    )(query, grad, key_values, key_values, enc_col, dec_row)


def spread_other_kernel(core_ref, gk_ref, gv_ref, w_ref, first_ref, second_ref):
    core = core_ref[0]
    width = gk_ref.shape[1]
    rows = pl.ds(pl.multiple_of((1 - core) * FB, FB), FB)
    out = lax.dot_general(gk_ref[...], w_ref[rows, :width], NT, preferred_element_type=jnp.float32)
    out = out + lax.dot_general(gv_ref[...], w_ref[rows, width:], NT, preferred_element_type=jnp.float32)
    out = out.astype(jnp.bfloat16).reshape(8, TB, FB)
    first_ref[:, 0] = out[:4]
    second_ref[:, 0] = out[4:]


def spread_other(core, grad_keys, grad_values, weight):
    rows, width = grad_keys.shape
    half = pl.BlockSpec((4, 1, TB, FB), lambda z, c: (0, z, 0, 0))
    whole = pl.BlockSpec((rows, width), lambda z, c: (0, 0))
    shape = jax.ShapeDtypeStruct((4, NZ, TB, FB), jnp.bfloat16)
    return pl.pallas_call(
        spread_other_kernel,
        grid_spec=pltpu.PrefetchScalarGridSpec(
            num_scalar_prefetch=1,
            grid=(NZ,),
            in_specs=[whole, whole, pl.BlockSpec((2 * FB, 2 * width), lambda z, c: (z, 0))],
            out_specs=[half, half],
        ),
        out_shape=[shape, shape],
        compiler_params=pltpu.CompilerParams(vmem_limit_bytes=VMEM),
        name="spread_other",
    )(core, grad_keys, grad_values, weight)


def spread_own_kernel(core_ref, gk_ref, gv_ref, w_ref, twin_ref, *out_refs):
    core = core_ref[0]
    width = gk_ref.shape[1]
    rows = pl.ds(pl.multiple_of(core * FB, FB), FB)
    out = lax.dot_general(gk_ref[...], w_ref[rows, :width], NT, preferred_element_type=jnp.float32)
    out = out + lax.dot_general(gv_ref[...], w_ref[rows, width:], NT, preferred_element_type=jnp.float32)
    out = out.reshape(4, TB, FB)
    for i in range(4):
        out_refs[i][0] = (out[i] + twin_ref[i, 0].astype(jnp.float32)).astype(jnp.bfloat16)


def spread_own(core, grad_keys, grad_values, weight, twin, which):
    rows, width = grad_keys.shape
    rows = rows // 2
    half = pl.BlockSpec((4, 1, TB, FB), lambda z, c: (0, z, 0, 0))
    part = pl.BlockSpec((rows, width), lambda z, c: (which, 0))
    shape = jax.ShapeDtypeStruct((NZ, TB, FB), jnp.bfloat16)
    return pl.pallas_call(
        spread_own_kernel,
        grid_spec=pltpu.PrefetchScalarGridSpec(
            num_scalar_prefetch=1,
            grid=(NZ,),
            in_specs=[part, part, pl.BlockSpec((2 * FB, 2 * width), lambda z, c: (z, 0)), half],
            out_specs=[pl.BlockSpec((1, TB, FB), lambda z, c: (z, 0, 0))] * 4,
        ),
        out_shape=[shape] * 4,
        compiler_params=pltpu.CompilerParams(vmem_limit_bytes=VMEM),
        name="spread_own",
    )(core, grad_keys, grad_values, weight, twin)


def shift(value, axis, size, by):
    return lax.ppermute(value, axis, [(i, (i + by) % size) for i in range(size)])


def total(parts):
    return functools.reduce(jnp.add, [p.astype(jnp.float32) for p in parts])


def per_device(enc_out, kv_weight, dec_query, ctx_grad, enc_seg, dec_seg):
    width = kv_weight.shape[3]
    weight = kv_weight[0].reshape(kv_weight.shape[1], 2 * width)
    core = lax.axis_index("c").reshape(1)
    x, y = lax.axis_index("x"), lax.axis_index("y")

    blocks = jnp.stack([((x + j) % NX) * NY + (1 - y if far else y) for far in (1, 0) for j in range(NX)])
    enc_col = enc_seg[0].reshape(8, TB)[blocks].reshape(8 * TB, 1)

    mine = enc_out[0]
    near = lax.all_to_all(jnp.broadcast_to(mine[None], (NZ, TB, FB)), "z", 0, 0)
    far = shift(near, "y", NY, 1)
    own = [far, None, None, None, near, None, None, None]
    for j in (2, 1, 3):
        own[4 + j] = shift(near, "x", NX, -j)
    for j in (2, 1, 3):
        own[j] = shift(far, "x", NX, -j)
    other = [shift(v, "c", NC, 1) for v in own]
    key_values = project(core, own, other, weight)

    context, grad_keys, grad_values = attend(dec_query[0, 0], ctx_grad[0, 0], key_values, enc_col, dec_seg)

    first, second = spread_other(core, grad_keys, grad_values, weight)
    first, second = shift(first, "c", NC, 1), shift(second, "c", NC, 1)
    away = spread_own(core, grad_keys, grad_values, weight, first, 0)
    home = spread_own(core, grad_keys, grad_values, weight, second, 1)
    away = [away[0]] + [shift(away[j], "x", NX, j) for j in (1, 2, 3)]
    home = [home[0]] + [shift(home[j], "x", NX, j) for j in (1, 2, 3)]
    crossed = shift(total(away).astype(jnp.bfloat16), "y", NY, 1)
    planes = total(home + [crossed]).astype(jnp.bfloat16)
    planes = lax.all_to_all(planes, "z", 0, 0)
    owned = jnp.sum(planes.astype(jnp.float32), axis=0)
    return context[None, None], owned[None]


def solution(mesh):
    fine = Mesh(mesh.devices.reshape(NZ, NC, NX, NY, ND), ("z", "c", "x", "y", "d"))
    section, mp = ("z", "c"), ("x", "y")
    placed = (
        P("d", mp, section),
        P(section, None, None, mp),
        P(section, "d", None, mp),
        P(section, "d", None, mp),
        P("d", None),
        P("d", None),
    )
    return jax.shard_map(
        per_device,
        mesh=fine,
        in_specs=placed,
        out_specs=(P(section, "d", None, mp), P("d", mp, section)),
        check_vma=False,
    )
```

```python
import functools

import jax
import jax.numpy as jnp
from jax import lax
from jax.experimental import pallas as pl
from jax.experimental.pallas import tpu as pltpu
from jax.sharding import Mesh, PartitionSpec as P

HD = 256
NZ, NC, NX, NY, ND = 8, 2, 4, 2, 2
TB = 64
FB = 256
NB = 8
VMEM = 40 << 20
AXES = ("z", "c", "x", "y")
NT = (((1,), (1,)), ((), ()))
TN = (((0,), (0,)), ((), ()))

Z_STEP = (0, 1, 2, 7)


def token_slot(b, i):
    return 2 * i + b


def z_slot(b, i):
    return (Z_STEP[i] + 4 * b) % NZ


def joint(value, move0, move1):
    pairs = []
    for z in range(NZ):
        for c in range(NC):
            for x in range(NX):
                for y in range(NY):
                    dz, dx, dy = (move0, move1)[c]
                    to = ((z + dz) % NZ, c, (x + dx) % NX, (y + dy) % NY)
                    flat = [((p[0] * NC + p[1]) * NX + p[2]) * NY + p[3] for p in ((z, c, x, y), to)]
                    pairs.append(tuple(flat))
    return lax.ppermute(value, AXES, pairs)


def small_stage(value, k, sign):
    return joint(value, (sign * k, 0, 0), (0, sign * (k >> 1), k & 1))


def across(value):
    return joint(value, (0, 0, 1), (4, 0, 0))


def big_stage(value, i, sign):
    return joint(value, (0, sign * i, 0), (sign * Z_STEP[i], 0, 0))


def twin(value):
    return lax.ppermute(value, "c", [(0, 1), (1, 0)])


def whole(n):
    return [pl.BlockSpec(memory_space=pltpu.VMEM)] * n


HBM = pl.BlockSpec(memory_space=pl.ANY)
SMEM = pl.BlockSpec(memory_space=pltpu.SMEM)


def project_kernel(place_ref, *refs):
    own, other, w_ref = refs[:8], refs[8:16], refs[16]
    out_ref, w_buf, lhs_ref, acc_ref, sems = refs[17:]
    z, core = place_ref[0], place_ref[1]
    rows = 2 * FB

    def load(k):
        start = pl.multiple_of(((z + k) % NZ) * rows, rows)
        return pltpu.make_async_copy(w_ref.at[pl.ds(start, rows), :], w_buf.at[pl.ds(k * rows, rows), :], sems.at[k])

    for k in range(NZ):
        load(k).start()

    def lay(even, odd):
        for b in range(2):
            for i in range(4):
                t = token_slot(b, i)
                for k in range(NZ):
                    lhs_ref[t * TB:(t + 1) * TB, k * rows:k * rows + FB] = even[4 * b + i][k]
                k = z_slot(b, i)
                lhs_ref[:, k * rows + FB:(k + 1) * rows] = odd[4 * b + i][...].reshape(8 * TB, FB)

    @pl.when(core == 0)
    def _():
        lay(own, other)

    @pl.when(core == 1)
    def _():
        lay(other, own)

    for k in range(0, NZ, 2):
        load(k).wait()
        load(k + 1).wait()
        span = pl.ds(k * rows, 2 * rows)
        part = jnp.dot(lhs_ref[:, span], w_buf[span, :], preferred_element_type=jnp.float32)
        if k == 0:
            acc_ref[...] = part
        elif k < NZ - 2:
            acc_ref[...] = acc_ref[...] + part
        else:
            out_ref[...] = (acc_ref[...] + part).astype(jnp.bfloat16)


def project(place, own, other, weight):
    depth, width = weight.shape
    rows = 8 * TB
    return pl.pallas_call(
        project_kernel,
        in_specs=[SMEM] + whole(16) + [HBM],
        out_specs=whole(1)[0],
        scratch_shapes=[
            pltpu.VMEM((depth, width), jnp.bfloat16),
            pltpu.VMEM((rows, depth), jnp.bfloat16),
            pltpu.VMEM((rows, width), jnp.float32),
            pltpu.SemaphoreType.DMA((NZ,)),
        ],
        out_shape=jax.ShapeDtypeStruct((rows, width), jnp.bfloat16),
        compiler_params=pltpu.CompilerParams(vmem_limit_bytes=VMEM),
        name="project",
    )(place, *own, *other, weight)


def attend_kernel(q_ref, g_ref, k_ref, v_ref, es_ref, ds_ref, ctx_ref, gk_ref, gv_ref):
    scale = HD ** -0.5
    q, g, k, v = q_ref[...], g_ref[...], k_ref[...], v_ref[...]
    same = es_ref[...] == ds_ref[...]
    scores = lax.dot_general(k, q, NT, preferred_element_type=jnp.float32) * scale
    scores = jnp.where(same, scores, -1e30)
    top = jnp.max(scores, axis=0, keepdims=True)
    raised = jnp.exp(scores - top)
    probs = raised / jnp.sum(raised, axis=0, keepdims=True)
    low = probs.astype(jnp.bfloat16)
    ctx_ref[...] = lax.dot_general(low, v, TN, preferred_element_type=jnp.float32).astype(jnp.bfloat16)
    gv_ref[...] = jnp.dot(low, g, preferred_element_type=jnp.float32).astype(jnp.bfloat16)
    gp = lax.dot_general(v, g, NT, preferred_element_type=jnp.float32)
    inner = jnp.sum(probs * gp, axis=0, keepdims=True)
    gs = (probs * (gp - inner) * scale).astype(jnp.bfloat16)
    gk_ref[...] = jnp.dot(gs, q, preferred_element_type=jnp.float32).astype(jnp.bfloat16)


def attend(query, grad, key_values, enc_col, dec_row):
    dec, width = query.shape
    enc = key_values.shape[0]
    heads = width // HD
    head = pl.BlockSpec((dec, HD), lambda h: (0, h))
    key = pl.BlockSpec((enc, HD), lambda h: (0, h))
    value = pl.BlockSpec((enc, HD), lambda h: (0, heads + h))
    return pl.pallas_call(
        attend_kernel,
        grid=(heads,),
        in_specs=[head, head, key, value, pl.BlockSpec((enc, 1), lambda h: (0, 0)), pl.BlockSpec((1, dec), lambda h: (0, 0))],
        out_specs=[head, key, key],
        out_shape=[
            jax.ShapeDtypeStruct((dec, width), jnp.bfloat16),
            jax.ShapeDtypeStruct((enc, width), jnp.bfloat16),
            jax.ShapeDtypeStruct((enc, width), jnp.bfloat16),
        ],
        compiler_params=pltpu.CompilerParams(vmem_limit_bytes=VMEM),
        name="attend",
    )(query, grad, key_values, key_values, enc_col, dec_row)


def spread_kernel(flip, place_ref, gk_ref, gv_ref, w_ref, home_ref, away_ref, w_buf, sems):
    z, core = place_ref[0], place_ref[1]
    parity = 1 - core if flip else core
    width = gk_ref.shape[1]
    outs = (home_ref, away_ref)

    def load(k):
        start = pl.multiple_of(((z + k) % NZ) * (2 * FB) + parity * FB, FB)
        return pltpu.make_async_copy(w_ref.at[pl.ds(start, FB), :], w_buf.at[k], sems.at[k])

    for k in range(NZ):
        load(k).start()
    for k in range(NZ):
        load(k).wait()
        out = lax.dot_general(gk_ref[...], w_buf[k, :, :width], NT, preferred_element_type=jnp.float32)
        out = out + lax.dot_general(gv_ref[...], w_buf[k, :, width:], NT, preferred_element_type=jnp.float32)
        out = out.astype(jnp.bfloat16).reshape(8, TB, FB)

        @pl.when(parity == 0)
        def _():
            for b in range(2):
                for i in range(4):
                    outs[b][i, k] = out[token_slot(b, i)]

        @pl.when(parity == 1)
        def _():
            b, i = [(b, i) for b in range(2) for i in range(4) if z_slot(b, i) == k][0]
            outs[b][i] = out


def spread(place, grad_keys, grad_values, weight, flip):
    shape = jax.ShapeDtypeStruct((4, NB, TB, FB), jnp.bfloat16)
    return pl.pallas_call(
        functools.partial(spread_kernel, flip),
        in_specs=[SMEM] + whole(2) + [HBM],
        out_specs=whole(2),
        scratch_shapes=[pltpu.VMEM((NZ, FB, weight.shape[1]), jnp.bfloat16), pltpu.SemaphoreType.DMA((NZ,))],
        out_shape=[shape] * 2,
        compiler_params=pltpu.CompilerParams(vmem_limit_bytes=VMEM),
        name="spread_other" if flip else "spread_own",
    )(place, grad_keys, grad_values, weight)


def merge_kernel(one_ref, two_ref, *out_refs):
    for i in range(4):
        out_refs[i][...] = (one_ref[i].astype(jnp.float32) + two_ref[i].astype(jnp.float32)).astype(jnp.bfloat16)


def merge(one, two):
    shape = jax.ShapeDtypeStruct((NB, TB, FB), jnp.bfloat16)
    return pl.pallas_call(
        merge_kernel,
        in_specs=whole(2),
        out_specs=whole(4),
        out_shape=[shape] * 4,
        compiler_params=pltpu.CompilerParams(vmem_limit_bytes=VMEM),
        name="merge",
    )(one, two)


def total(parts):
    return functools.reduce(jnp.add, [p.astype(jnp.float32) for p in parts])


FAR_FIRST = (4, 5, 3, 6, 2, 7, 1)


def per_device(enc_out, kv_weight, dec_query, ctx_grad, enc_seg, dec_seg):
    width = kv_weight.shape[3]
    z, core, x, y = (lax.axis_index(a) for a in AXES)
    place = jnp.stack([z, core])

    mine = enc_out[0]
    slots = [mine] + [None] * 7
    for k in FAR_FIRST:
        slots[k] = small_stage(mine, k, -1)
    near = jnp.stack(slots)
    weight = kv_weight[0].reshape(kv_weight.shape[1], 2 * width)

    blocks = jnp.stack([((x + k // 2) % NX) * NY + (y + k % 2) % NY for k in range(8)])
    enc_col = enc_seg[0].reshape(8, TB)[blocks].reshape(8 * TB, 1)

    far = across(near)
    own = [near] + [big_stage(near, i, -1) for i in (2, 1, 3)] + [far] + [big_stage(far, i, -1) for i in (2, 1, 3)]
    own = [own[0], own[2], own[1], own[3], own[4], own[6], own[5], own[7]]
    other = [twin(v) for v in own]
    key_values = project(place, own, other, weight)

    context, grad_keys, grad_values = attend(dec_query[0, 0], ctx_grad[0, 0], key_values, enc_col, dec_seg)

    home, away = spread(place, grad_keys, grad_values, weight, True)
    away, home = twin(away), twin(home)
    own_home, own_away = spread(place, grad_keys, grad_values, weight, False)
    away = merge(own_away, away)
    away = [away[0]] + [big_stage(away[i], i, 1) for i in (2, 1, 3)]
    home = merge(own_home, home)
    home = [home[0]] + [big_stage(home[i], i, 1) for i in (2, 1, 3)]
    crossed = across(total(away).astype(jnp.bfloat16))
    planes = total(home + [crossed]).astype(jnp.bfloat16)
    owned = total([planes[0]] + [small_stage(planes[k], k, 1) for k in FAR_FIRST])
    return context[None, None], owned[None]


def solution(mesh):
    fine = Mesh(mesh.devices.reshape(NZ, NC, NX, NY, ND), ("z", "c", "x", "y", "d"))
    section, mp = ("z", "c"), ("x", "y")
    placed = (
        P("d", mp, section),
        P(section, None, None, mp),
        P(section, "d", None, mp),
        P(section, "d", None, mp),
        P("d", None),
        P("d", None),
    )
    return jax.shard_map(
        per_device,
        mesh=fine,
        in_specs=placed,
        out_specs=(P(section, "d", None, mp), P("d", mp, section)),
        check_vma=False,
    )
```

```python
import functools

import jax
import jax.numpy as jnp
from jax import lax
from jax.experimental import pallas as pl
from jax.experimental.pallas import tpu as pltpu
from jax.sharding import Mesh, PartitionSpec as P

HD = 256
NZ, NC, NX, NY, ND = 8, 2, 4, 2, 2
TB = 64
FB = 256
NB = 8
VMEM = 24 << 20
AXES = ("z", "c", "x", "y")
NT = (((1,), (1,)), ((), ()))
TN = (((0,), (0,)), ((), ()))

Z_STEP = (0, 1, 2, 7)


def flat(z, c, x, y):
    return ((z * NC + c) * NX + x) * NY + y


SMALL_GROUPS = [[flat(z, 0, x, y) for z in range(NZ)] for x in range(NX) for y in range(NY)]
SMALL_GROUPS += [[flat(z, 1, x, y) for x in range(NX) for y in range(NY)] for z in range(NZ)]


def small_stage(value):
    return lax.all_to_all(value, AXES, 0, 0, axis_index_groups=SMALL_GROUPS)


def joint(value, move0, move1):
    pairs = []
    for z in range(NZ):
        for c in range(NC):
            for x in range(NX):
                for y in range(NY):
                    dz, dx, dy = (move0, move1)[c]
                    pairs.append((flat(z, c, x, y), flat((z + dz) % NZ, c, (x + dx) % NX, (y + dy) % NY)))
    return lax.ppermute(value, AXES, pairs)


def across(value):
    return joint(value, (0, 0, 1), (4, 0, 0))


def big_stage(value, i, sign):
    return joint(value, (0, sign * i, 0), (sign * Z_STEP[i], 0, 0))


def twin(value):
    return lax.ppermute(value, "c", [(0, 1), (1, 0)])


def whole(n):
    return [pl.BlockSpec(memory_space=pltpu.VMEM)] * n


HBM = pl.BlockSpec(memory_space=pltpu.HBM)
SMEM = pl.BlockSpec(memory_space=pltpu.SMEM)


def project_kernel(place_ref, *refs):
    own, other, w_ref = refs[:8], refs[8:16], refs[16]
    out_ref, w_buf, lhs_ref, acc_ref, sems = refs[17:]
    z, core, x, y = place_ref[0], place_ref[1], place_ref[2], place_ref[3]
    rows = 4 * FB

    def load(k):
        span = pl.ds(k * rows, rows)
        return pltpu.make_async_copy(w_ref.at[span, :], w_buf.at[span, :], sems.at[k])

    for k in range(4):
        load(k).start()

    def lay(even, odd):
        for b in range(2):
            for i in range(4):
                start = pl.multiple_of((((x + i) % NX) * NY + (y + b) % NY) * TB, TB)
                for k in range(NZ):
                    lhs_ref[2 * k, pl.ds(start, TB), :] = even[4 * b + i][k]
                lhs_ref[2 * ((z + Z_STEP[i] + 4 * b) % NZ) + 1] = odd[4 * b + i][...].reshape(NB * TB, FB)

    @pl.when(core == 0)
    def _():
        lay(own, other)

    @pl.when(core == 1)
    def _():
        lay(other, own)

    for k in range(4):
        load(k).wait()
        lhs = jnp.concatenate([lhs_ref[4 * k + n] for n in range(4)], axis=1)
        part = jnp.dot(lhs, w_buf[pl.ds(k * rows, rows), :], preferred_element_type=jnp.float32)
        if k == 0:
            acc_ref[...] = part
        elif k < 3:
            acc_ref[...] = acc_ref[...] + part
        else:
            out_ref[...] = (acc_ref[...] + part).astype(jnp.bfloat16)


def project(place, own, other, weight):
    depth, width = weight.shape
    rows = NB * TB
    return pl.pallas_call(
        project_kernel,
        in_specs=[SMEM] + whole(16) + [HBM],
        out_specs=whole(1)[0],
        scratch_shapes=[
            pltpu.VMEM((depth, width), jnp.bfloat16),
            pltpu.VMEM((2 * NZ, rows, FB), jnp.bfloat16),
            pltpu.VMEM((rows, width), jnp.float32),
            pltpu.SemaphoreType.DMA((4,)),
        ],
        out_shape=jax.ShapeDtypeStruct((rows, width), jnp.bfloat16),
        compiler_params=pltpu.CompilerParams(vmem_limit_bytes=VMEM),
        name="project",
    )(place, *own, *other, weight)


def attend_kernel(q_ref, g_ref, k_ref, v_ref, es_ref, ds_ref, ctx_ref, gk_ref, gv_ref):
    scale = HD ** -0.5
    q, g, k, v = q_ref[...], g_ref[...], k_ref[...], v_ref[...]
    same = es_ref[...] == ds_ref[...]
    scores = lax.dot_general(k, q, NT, preferred_element_type=jnp.float32) * scale
    scores = jnp.where(same, scores, -1e30)
    top = jnp.max(scores, axis=0, keepdims=True)
    raised = jnp.exp(scores - top)
    probs = raised / jnp.sum(raised, axis=0, keepdims=True)
    low = probs.astype(jnp.bfloat16)
    ctx_ref[...] = lax.dot_general(low, v, TN, preferred_element_type=jnp.float32).astype(jnp.bfloat16)
    gv_ref[...] = jnp.dot(low, g, preferred_element_type=jnp.float32).astype(jnp.bfloat16)
    gp = lax.dot_general(v, g, NT, preferred_element_type=jnp.float32)
    inner = jnp.sum(probs * gp, axis=0, keepdims=True)
    gs = (probs * (gp - inner) * scale).astype(jnp.bfloat16)
    gk_ref[...] = jnp.dot(gs, q, preferred_element_type=jnp.float32).astype(jnp.bfloat16)


def attend(query, grad, key_values, enc_col, dec_row):
    dec, width = query.shape
    enc = key_values.shape[0]
    heads = width // HD
    head = pl.BlockSpec((dec, HD), lambda h: (0, h))
    key = pl.BlockSpec((enc, HD), lambda h: (0, h))
    value = pl.BlockSpec((enc, HD), lambda h: (0, heads + h))
    return pl.pallas_call(
        attend_kernel,
        grid=(heads,),
        in_specs=[head, head, key, value, pl.BlockSpec((enc, 1), lambda h: (0, 0)), pl.BlockSpec((1, dec), lambda h: (0, 0))],
        out_specs=[head, key, key],
        out_shape=[
            jax.ShapeDtypeStruct((dec, width), jnp.bfloat16),
            jax.ShapeDtypeStruct((enc, width), jnp.bfloat16),
            jax.ShapeDtypeStruct((enc, width), jnp.bfloat16),
        ],
        compiler_params=pltpu.CompilerParams(vmem_limit_bytes=VMEM),
        name="attend",
    )(query, grad, key_values, key_values, enc_col, dec_row)


def spread_kernel(flip, place_ref, gk_ref, gv_ref, w_ref, out_ref, w_buf, sems):
    z, core, x, y = place_ref[0], place_ref[1], place_ref[2], place_ref[3]
    parity = 1 - core if flip else core
    width = gk_ref.shape[1]

    def load(k):
        start = pl.multiple_of(k * (2 * FB) + parity * FB, FB)
        return pltpu.make_async_copy(w_ref.at[pl.ds(start, FB), :], w_buf.at[k], sems.at[k])

    def place_out(k, out):
        @pl.when(parity == 0)
        def _():
            for m in range(NB):
                out_ref[(m + y) % NY, (m // NY + NX - x) % NX, k] = out[m]

        @pl.when(parity == 1)
        def _():
            away = (k + NZ - z) % NZ
            i = away % 4
            out_ref[(away // 4 + i // 3) % 2, i] = out

    for k in range(NZ):
        load(k).start()
    grads = jnp.concatenate([gk_ref[...], gv_ref[...]], axis=1)
    for k in range(0, NZ, 2):
        load(k).wait()
        load(k + 1).wait()
        rows = w_buf[pl.ds(k, 2)].reshape(2 * FB, 2 * width)
        out = lax.dot_general(grads, rows, NT, preferred_element_type=jnp.float32).astype(jnp.bfloat16)
        for n in range(2):
            place_out(k + n, out[:, n * FB:(n + 1) * FB].reshape(NB, TB, FB))


def spread(place, grad_keys, grad_values, weight, flip):
    return pl.pallas_call(
        functools.partial(spread_kernel, flip),
        in_specs=[SMEM] + whole(2) + [HBM],
        out_specs=whole(1)[0],
        scratch_shapes=[pltpu.VMEM((NZ, FB, weight.shape[1]), jnp.bfloat16), pltpu.SemaphoreType.DMA((NZ,))],
        out_shape=jax.ShapeDtypeStruct((2, 4, NB, TB, FB), jnp.bfloat16),
        compiler_params=pltpu.CompilerParams(vmem_limit_bytes=VMEM),
        name="spread_other" if flip else "spread_own",
    )(place, grad_keys, grad_values, weight)


def merge_kernel(one_ref, two_ref, *out_refs):
    for b in range(2):
        for i in range(4):
            both = one_ref[b, i].astype(jnp.float32) + two_ref[b, i].astype(jnp.float32)
            out_refs[4 * b + i][...] = both.astype(jnp.bfloat16)


def merge(one, two):
    shape = jax.ShapeDtypeStruct((NB, TB, FB), jnp.bfloat16)
    return pl.pallas_call(
        merge_kernel,
        in_specs=whole(2),
        out_specs=whole(8),
        out_shape=[shape] * 8,
        compiler_params=pltpu.CompilerParams(vmem_limit_bytes=VMEM),
        name="merge",
    )(one, two)


def total(parts):
    return functools.reduce(jnp.add, [p.astype(jnp.float32) for p in parts])


def per_device(enc_out, kv_weight, dec_query, ctx_grad, enc_seg, dec_seg):
    width = kv_weight.shape[3]
    place = jnp.stack([lax.axis_index(a) for a in AXES])

    near = small_stage(jnp.broadcast_to(enc_out, (NB, TB, FB)))
    far = across(near)
    own = [near] + [big_stage(near, i, -1) for i in (1, 2, 3)]
    far, *own, kv_weight = lax.optimization_barrier((far, *own, kv_weight))
    own += [far] + [big_stage(far, i, -1) for i in (1, 2, 3)]
    weight = kv_weight[0].reshape(kv_weight.shape[1], 2 * width)
    weight = pltpu.with_memory_space_constraint(weight, pltpu.HBM)
    *own[:5], weight = lax.optimization_barrier((*own[:5], weight))
    other = [twin(v) for v in own]
    key_values = project(place, own, other, weight)

    enc_col = enc_seg.reshape(NB * TB, 1)
    context, grad_keys, grad_values = attend(dec_query[0, 0], ctx_grad[0, 0], key_values, enc_col, dec_seg)

    theirs = twin(spread(place, grad_keys, grad_values, weight, True))
    mine = spread(place, grad_keys, grad_values, weight, False)
    parts = merge(mine, theirs)
    away = [parts[4]] + [big_stage(parts[4 + i], i, 1) for i in (1, 2, 3)]
    home = [parts[0]] + [big_stage(parts[i], i, 1) for i in (1, 2, 3)]
    crossed = across(total(away).astype(jnp.bfloat16))
    planes = total(home + [crossed]).astype(jnp.bfloat16)
    owned = jnp.sum(small_stage(planes).astype(jnp.float32), axis=0)
    return context[None, None], owned[None]


def solution(mesh):
    fine = Mesh(mesh.devices.reshape(NZ, NC, NX, NY, ND), ("z", "c", "x", "y", "d"))
    section, mp = ("z", "c"), ("x", "y")
    placed = (
        P("d", mp, section),
        P(section, None, None, mp),
        P(section, "d", None, mp),
        P(section, "d", None, mp),
        P("d", None),
        P("d", None),
    )
    return jax.shard_map(
        per_device,
        mesh=fine,
        in_specs=placed,
        out_specs=(P(section, "d", None, mp), P("d", mp, section)),
        check_vma=False,
    )
```

```python
import functools

import jax
import jax.numpy as jnp
from jax import lax
from jax.experimental import pallas as pl
from jax.experimental.pallas import tpu as pltpu
from jax.sharding import Mesh, PartitionSpec as P

HD = 256
NZ, NC, NX, NY, ND = 8, 2, 4, 2, 2
TB = 64
FB = 256
NB = 8
VMEM = 20 << 20
AXES = ("z", "c", "x", "y")
NT = (((1,), (1,)), ((), ()))
TN = (((0,), (0,)), ((), ()))

Z_STEP = (0, 1, 2, 7)


def flat(z, c, x, y):
    return ((z * NC + c) * NX + x) * NY + y


SMALL_GROUPS = [[flat(z, 0, x, y) for z in range(NZ)] for x in range(NX) for y in range(NY)]
SMALL_GROUPS += [[flat(z, 1, x, y) for x in range(NX) for y in range(NY)] for z in range(NZ)]


def small_stage(value):
    return lax.all_to_all(value, AXES, 0, 0, axis_index_groups=SMALL_GROUPS)


def joint(value, move0, move1):
    pairs = []
    for z in range(NZ):
        for c in range(NC):
            for x in range(NX):
                for y in range(NY):
                    dz, dx, dy = (move0, move1)[c]
                    pairs.append((flat(z, c, x, y), flat((z + dz) % NZ, c, (x + dx) % NX, (y + dy) % NY)))
    return lax.ppermute(value, AXES, pairs)


def across(value):
    return joint(value, (0, 0, 1), (4, 0, 0))


def big_stage(value, i, sign):
    return joint(value, (0, sign * i, 0), (sign * Z_STEP[i], 0, 0))


def twin(value):
    return lax.ppermute(value, "c", [(0, 1), (1, 0)])


def whole(n):
    return [pl.BlockSpec(memory_space=pltpu.VMEM)] * n


HBM = pl.BlockSpec(memory_space=pltpu.HBM)
SMEM = pl.BlockSpec(memory_space=pltpu.SMEM)


def relayout_kernel(w_ref, out_ref, mark_ref, raw_ref, done_ref, load_sems, store_sems):
    def load(k):
        return pltpu.make_async_copy(w_ref.at[0, pl.ds(k * NC * FB, NC * FB)], raw_ref.at[k], load_sems.at[k])

    def store(k):
        return pltpu.make_async_copy(done_ref.at[k], out_ref.at[k], store_sems.at[k])

    for k in range(NZ):
        load(k).start()
    mark_ref[...] = jnp.zeros(mark_ref.shape, mark_ref.dtype)
    for k in range(NZ):
        load(k).wait()
        done_ref[k] = raw_ref[k].reshape(done_ref.shape[1:])
        store(k).start()
    for k in range(NZ):
        store(k).wait()


def relayout(weight):
    width = weight.shape[3]
    shape = (NZ, NC, FB, 2 * width)
    return pl.pallas_call(
        relayout_kernel,
        in_specs=[HBM],
        out_specs=[HBM] + whole(1),
        scratch_shapes=[
            pltpu.VMEM((NZ, NC * FB, 2, width), jnp.bfloat16),
            pltpu.VMEM(shape, jnp.bfloat16),
            pltpu.SemaphoreType.DMA((NZ,)),
            pltpu.SemaphoreType.DMA((NZ,)),
        ],
        out_shape=[pltpu.HBM(shape, jnp.bfloat16), jax.ShapeDtypeStruct((8, 128), jnp.float32)],
        compiler_params=pltpu.CompilerParams(vmem_limit_bytes=20 << 20),
        name="relayout",
    )(weight)


def lay_out(out_ref, parity, z, x, y, k, out):
    @pl.when(parity == 0)
    def _():
        for m in range(NB):
            out_ref[(m + y) % NY, (m // NY + NX - x) % NX, k] = out[m]

    @pl.when(parity == 1)
    def _():
        away = (k + NZ - z) % NZ
        i = away % 4
        out_ref[(away // 4 + i // 3) % 2, i] = out


def load_weights(w_ref, w_buf, sems, k, core, slot):
    return pltpu.make_async_copy(w_ref.at[k, core], w_buf.at[k, slot], sems.at[k, slot])


def spread(grads, w_buf, slot, out_ref, parity, z, x, y, ready):
    for k in range(0, NZ, 2):
        ready(k)
        ready(k + 1)
        rows = w_buf[pl.ds(k, 2), slot].reshape(2 * FB, grads.shape[1])
        out = lax.dot_general(grads, rows, NT, preferred_element_type=jnp.float32).astype(jnp.bfloat16)
        for n in range(2):
            lay_out(out_ref, parity, z, x, y, k + n, out[:, n * FB:(n + 1) * FB].reshape(NB, TB, FB))


def attend(q, g, k, v, same):
    scale = HD ** -0.5
    scores = lax.dot_general(k, q, NT, preferred_element_type=jnp.float32) * scale
    scores = jnp.where(same, scores, -1e30)
    top = jnp.max(scores, axis=0, keepdims=True)
    raised = jnp.exp(scores - top)
    probs = raised / jnp.sum(raised, axis=0, keepdims=True)
    low = probs.astype(jnp.bfloat16)
    context = lax.dot_general(low, v, TN, preferred_element_type=jnp.float32).astype(jnp.bfloat16)
    grad_values = jnp.dot(low, g, preferred_element_type=jnp.float32).astype(jnp.bfloat16)
    gp = lax.dot_general(v, g, NT, preferred_element_type=jnp.float32)
    inner = jnp.sum(probs * gp, axis=0, keepdims=True)
    gs = (probs * (gp - inner) * scale).astype(jnp.bfloat16)
    grad_keys = jnp.dot(gs, q, preferred_element_type=jnp.float32).astype(jnp.bfloat16)
    return context, grad_keys, grad_values


def main_kernel(place_ref, *refs):
    own, other = refs[:8], refs[8:16]
    w_ref, _, q_ref, g_ref, es_ref, ds_ref, ctx_ref, grad_ref, out_ref, w_buf, lhs_ref, acc_ref, kv_ref, sems = refs[16:]
    z, core, x, y = place_ref[0], place_ref[1], place_ref[2], place_ref[3]
    dec, width = q_ref.shape
    enc = NB * TB

    for k in range(NZ):
        for c in range(NC):
            load_weights(w_ref, w_buf, sems, k, c, c).start()

    def lay(even, odd):
        for b in range(2):
            for i in range(4):
                start = pl.multiple_of((((x + i) % NX) * NY + (y + b) % NY) * TB, TB)
                for k in range(NZ):
                    lhs_ref[2 * k, pl.ds(start, TB), :] = even[4 * b + i][k]
                lhs_ref[2 * ((z + Z_STEP[i] + 4 * b) % NZ) + 1] = odd[4 * b + i][...].reshape(enc, FB)

    @pl.when(core == 0)
    def _():
        lay(own, other)

    @pl.when(core == 1)
    def _():
        lay(other, own)

    for k in range(0, NZ, 2):
        for n in range(4):
            load_weights(w_ref, w_buf, sems, k + n // 2, n % 2, n % 2).wait()
        lhs = jnp.concatenate([lhs_ref[2 * k + n] for n in range(4)], axis=1)
        rows = w_buf[pl.ds(k, 2)].reshape(4 * FB, 2 * width)
        part = jnp.dot(lhs, rows, preferred_element_type=jnp.float32)
        if k == 0:
            acc_ref[...] = part
        elif k < NZ - 2:
            acc_ref[...] = acc_ref[...] + part
        else:
            kv_ref[...] = (acc_ref[...] + part).astype(jnp.bfloat16)

    same = es_ref[...] == ds_ref[...]
    for h in range(width // HD):
        head = pl.ds(h * HD, HD)
        value = pl.ds(width + h * HD, HD)
        found = attend(q_ref[:, head], g_ref[:, head], kv_ref[:, head], kv_ref[:, value], same)
        ctx_ref[:, head], grad_ref[:, head], grad_ref[:, value] = found

    spread(grad_ref[...], w_buf, 1 - core, out_ref, 1 - core, z, x, y, lambda k: None)


def main(place, own, other, weight, mark, query, grad, enc_col, dec_row):
    dec, width = query.shape
    enc = NB * TB
    return pl.pallas_call(
        main_kernel,
        in_specs=[SMEM] + whole(16) + [HBM] + whole(5),
        out_specs=whole(3),
        scratch_shapes=[
            pltpu.VMEM((NZ, NC, FB, 2 * width), jnp.bfloat16),
            pltpu.VMEM((2 * NZ, enc, FB), jnp.bfloat16),
            pltpu.VMEM((enc, 2 * width), jnp.float32),
            pltpu.VMEM((enc, 2 * width), jnp.bfloat16),
            pltpu.SemaphoreType.DMA((NZ, NC)),
        ],
        out_shape=[
            jax.ShapeDtypeStruct((dec, width), jnp.bfloat16),
            jax.ShapeDtypeStruct((enc, 2 * width), jnp.bfloat16),
            jax.ShapeDtypeStruct((2, 4, NB, TB, FB), jnp.bfloat16),
        ],
        compiler_params=pltpu.CompilerParams(vmem_limit_bytes=28 << 20),
        name="main",
    )(place, *own, *other, weight, mark, query, grad, enc_col, dec_row)


def own_kernel(place_ref, grad_ref, w_ref, out_ref, w_buf, sems):
    z, core, x, y = place_ref[0], place_ref[1], place_ref[2], place_ref[3]
    for k in range(NZ):
        load_weights(w_ref, w_buf, sems, k, core, 0).start()
    ready = lambda k: load_weights(w_ref, w_buf, sems, k, core, 0).wait()
    spread(grad_ref[...], w_buf, 0, out_ref, core, z, x, y, ready)


def spread_own(place, grads, weight):
    return pl.pallas_call(
        own_kernel,
        in_specs=[SMEM] + whole(1) + [HBM],
        out_specs=whole(1)[0],
        scratch_shapes=[pltpu.VMEM((NZ, 1, FB, grads.shape[1]), jnp.bfloat16), pltpu.SemaphoreType.DMA((NZ, 1))],
        out_shape=jax.ShapeDtypeStruct((2, 4, NB, TB, FB), jnp.bfloat16),
        compiler_params=pltpu.CompilerParams(vmem_limit_bytes=VMEM),
        name="spread_own",
    )(place, grads, weight)


def merge_kernel(one_ref, two_ref, *out_refs):
    for b in range(2):
        for i in range(4):
            both = one_ref[b, i].astype(jnp.float32) + two_ref[b, i].astype(jnp.float32)
            out_refs[4 * b + i][...] = both.astype(jnp.bfloat16)


def merge(one, two):
    shape = jax.ShapeDtypeStruct((NB, TB, FB), jnp.bfloat16)
    return pl.pallas_call(
        merge_kernel,
        in_specs=whole(2),
        out_specs=whole(8),
        out_shape=[shape] * 8,
        compiler_params=pltpu.CompilerParams(vmem_limit_bytes=VMEM),
        name="merge",
    )(one, two)


def total(parts):
    return functools.reduce(jnp.add, [p.astype(jnp.float32) for p in parts])


def per_device(enc_out, kv_weight, dec_query, ctx_grad, enc_seg, dec_seg):
    width = kv_weight.shape[3]
    place = jnp.stack([lax.axis_index(a) for a in AXES])

    near = small_stage(jnp.broadcast_to(enc_out, (NB, TB, FB)))
    far = across(near)
    own = [near] + [big_stage(near, i, -1) for i in (1, 2, 3)]
    far, own[1], kv_weight = lax.optimization_barrier((far, own[1], kv_weight))
    weight, mark = relayout(pltpu.with_memory_space_constraint(kv_weight, pltpu.HBM))
    weight = pltpu.with_memory_space_constraint(weight, pltpu.HBM)
    own += [far] + [big_stage(far, i, -1) for i in (1, 2, 3)]
    *own[:5], mark = lax.optimization_barrier((*own[:5], mark))
    other = [pltpu.with_memory_space_constraint(twin(v), pltpu.HBM) for v in own]

    enc_col = enc_seg.reshape(NB * TB, 1)
    context, grads, theirs = main(place, own, other, weight, mark, dec_query[0, 0], ctx_grad[0, 0], enc_col, dec_seg)
    theirs = twin(theirs)
    mine = spread_own(place, grads, weight)
    parts = merge(mine, theirs)
    away = [parts[4]] + [big_stage(parts[4 + i], i, 1) for i in (1, 2, 3)]
    home = [parts[0]] + [big_stage(parts[i], i, 1) for i in (1, 2, 3)]
    crossed = across(total(away).astype(jnp.bfloat16))
    planes = total(home + [crossed]).astype(jnp.bfloat16)
    owned = jnp.sum(small_stage(planes).astype(jnp.float32), axis=0)
    return context[None, None], owned[None]


def solution(mesh):
    fine = Mesh(mesh.devices.reshape(NZ, NC, NX, NY, ND), ("z", "c", "x", "y", "d"))
    section, mp = ("z", "c"), ("x", "y")
    placed = (
        P("d", mp, section),
        P(section, None, None, mp),
        P(section, "d", None, mp),
        P(section, "d", None, mp),
        P("d", None),
        P("d", None),
    )
    return jax.shard_map(
        per_device,
        mesh=fine,
        in_specs=placed,
        out_specs=(P(section, "d", None, mp), P("d", mp, section)),
        check_vma=False,
    )
```

```python
import functools

import jax
import jax.numpy as jnp
from jax import lax
from jax.experimental import pallas as pl
from jax.experimental.pallas import tpu as pltpu
from jax.sharding import Mesh, PartitionSpec as P

HD = 256
NZ, NC, NX, NY, ND = 8, 2, 4, 2, 2
TB = 64
FB = 256
NB = 8
VMEM = 20 << 20
AXES = ("z", "c", "x", "y")
NT = (((1,), (1,)), ((), ()))
TN = (((0,), (0,)), ((), ()))

Z_STEP = (0, 1, 2, 7)


def flat(z, c, x, y):
    return ((z * NC + c) * NX + x) * NY + y


SMALL_GROUPS = [[flat(z, 0, x, y) for z in range(NZ)] for x in range(NX) for y in range(NY)]
SMALL_GROUPS += [[flat(z, 1, x, y) for x in range(NX) for y in range(NY)] for z in range(NZ)]


def small_stage(value):
    return lax.all_to_all(value, AXES, 0, 0, axis_index_groups=SMALL_GROUPS)


def joint(value, move0, move1):
    pairs = []
    for z in range(NZ):
        for c in range(NC):
            for x in range(NX):
                for y in range(NY):
                    dz, dx, dy = (move0, move1)[c]
                    pairs.append((flat(z, c, x, y), flat((z + dz) % NZ, c, (x + dx) % NX, (y + dy) % NY)))
    return lax.ppermute(value, AXES, pairs)


def across(value):
    return joint(value, (0, 0, 1), (4, 0, 0))


def big_stage(value, i, sign):
    return joint(value, (0, sign * i, 0), (sign * Z_STEP[i], 0, 0))


def twin(value):
    return lax.ppermute(value, "c", [(0, 1), (1, 0)])


def whole(n):
    return [pl.BlockSpec(memory_space=pltpu.VMEM)] * n


HBM = pl.BlockSpec(memory_space=pltpu.HBM)
SMEM = pl.BlockSpec(memory_space=pltpu.SMEM)


def relayout_kernel(w_ref, out_ref, mark_ref, raw_ref, done_ref, load_sems, store_sems):
    def load(k):
        return pltpu.make_async_copy(w_ref.at[0, pl.ds(k * NC * FB, NC * FB)], raw_ref.at[k], load_sems.at[k])

    def store(k):
        return pltpu.make_async_copy(done_ref.at[k], out_ref.at[k], store_sems.at[k])

    for k in range(NZ):
        load(k).start()
    mark_ref[...] = jnp.zeros(mark_ref.shape, mark_ref.dtype)
    for k in range(NZ):
        load(k).wait()
        done_ref[k] = raw_ref[k].reshape(done_ref.shape[1:])
        store(k).start()
    for k in range(NZ):
        store(k).wait()


def relayout(weight):
    width = weight.shape[3]
    shape = (NZ, NC, FB, 2 * width)
    return pl.pallas_call(
        relayout_kernel,
        in_specs=[HBM],
        out_specs=[HBM] + whole(1),
        scratch_shapes=[
            pltpu.VMEM((NZ, NC * FB, 2, width), jnp.bfloat16),
            pltpu.VMEM(shape, jnp.bfloat16),
            pltpu.SemaphoreType.DMA((NZ,)),
            pltpu.SemaphoreType.DMA((NZ,)),
        ],
        out_shape=[pltpu.HBM(shape, jnp.bfloat16), jax.ShapeDtypeStruct((8, 128), jnp.float32)],
        compiler_params=pltpu.CompilerParams(vmem_limit_bytes=20 << 20),
        name="relayout",
    )(weight)


def lay_out(out_refs, parity, z, x, y, k, out):
    slot = (k + NZ - z) % NZ
    i = slot % 4
    b = (slot // 4 + i // 3) % 2
    for half in range(2):

        @pl.when((parity == 0) & (y == half))
        def _():
            for m in range(NB):
                out_refs[(m + half) % NY][(m // NY + NX - x) % NX, k] = out[m]

        @pl.when((parity == 1) & (b == half))
        def _():
            out_refs[half][i] = out


def load_weights(w_ref, w_buf, sems, k, core, slot):
    return pltpu.make_async_copy(w_ref.at[k, core], w_buf.at[k, slot], sems.at[k, slot])


def spread(grads, w_buf, slot, out_refs, parity, z, x, y):
    for k in range(0, NZ, 2):
        rows = w_buf[pl.ds(k, 2), slot].reshape(2 * FB, grads.shape[1])
        out = lax.dot_general(grads, rows, NT, preferred_element_type=jnp.float32).astype(jnp.bfloat16)
        for n in range(2):
            lay_out(out_refs, parity, z, x, y, k + n, out[:, n * FB:(n + 1) * FB].reshape(NB, TB, FB))


def attend(q, g, k, v, same):
    scale = HD ** -0.5
    scores = lax.dot_general(k, q, NT, preferred_element_type=jnp.float32) * scale
    scores = jnp.where(same, scores, -1e30)
    top = jnp.max(scores, axis=0, keepdims=True)
    raised = jnp.exp(scores - top)
    probs = raised / jnp.sum(raised, axis=0, keepdims=True)
    low = probs.astype(jnp.bfloat16)
    context = lax.dot_general(low, v, TN, preferred_element_type=jnp.float32).astype(jnp.bfloat16)
    grad_values = jnp.dot(low, g, preferred_element_type=jnp.float32).astype(jnp.bfloat16)
    gp = lax.dot_general(v, g, NT, preferred_element_type=jnp.float32)
    inner = jnp.sum(probs * gp, axis=0, keepdims=True)
    gs = (probs * (gp - inner) * scale).astype(jnp.bfloat16)
    grad_keys = jnp.dot(gs, q, preferred_element_type=jnp.float32).astype(jnp.bfloat16)
    return context, grad_keys, grad_values


def main_kernel(place_ref, *refs):
    own, other = refs[:8], refs[8:16]
    w_ref, _, q_ref, g_ref, es_ref, ds_ref, ctx_ref, grad_ref, home_ref, away_ref, w_buf, lhs_ref, acc_ref, kv_ref, sems = refs[16:]
    z, core, x, y = place_ref[0], place_ref[1], place_ref[2], place_ref[3]
    dec, width = q_ref.shape
    enc = NB * TB

    for k in range(NZ):
        for c in range(NC):
            load_weights(w_ref, w_buf, sems, k, c, c).start()

    def lay(even, odd):
        for b in range(2):
            for i in range(4):
                start = pl.multiple_of((((x + i) % NX) * NY + (y + b) % NY) * TB, TB)
                for k in range(NZ):
                    lhs_ref[2 * k, pl.ds(start, TB), :] = even[4 * b + i][k]
                lhs_ref[2 * ((z + Z_STEP[i] + 4 * b) % NZ) + 1] = odd[4 * b + i][...].reshape(enc, FB)

    @pl.when(core == 0)
    def _():
        lay(own, other)

    @pl.when(core == 1)
    def _():
        lay(other, own)

    for k in range(0, NZ, 2):
        for n in range(4):
            load_weights(w_ref, w_buf, sems, k + n // 2, n % 2, n % 2).wait()
        lhs = jnp.concatenate([lhs_ref[2 * k + n] for n in range(4)], axis=1)
        rows = w_buf[pl.ds(k, 2)].reshape(4 * FB, 2 * width)
        part = jnp.dot(lhs, rows, preferred_element_type=jnp.float32)
        if k == 0:
            acc_ref[...] = part
        elif k < NZ - 2:
            acc_ref[...] = acc_ref[...] + part
        else:
            kv_ref[...] = (acc_ref[...] + part).astype(jnp.bfloat16)

    same = es_ref[...] == ds_ref[...]
    for h in range(width // HD):
        head = pl.ds(h * HD, HD)
        value = pl.ds(width + h * HD, HD)
        found = attend(q_ref[:, head], g_ref[:, head], kv_ref[:, head], kv_ref[:, value], same)
        ctx_ref[:, head], grad_ref[:, head], grad_ref[:, value] = found

    spread(grad_ref[...], w_buf, 1 - core, (home_ref, away_ref), 1 - core, z, x, y)


def main(place, own, other, weight, mark, query, grad, enc_col, dec_row):
    dec, width = query.shape
    enc = NB * TB
    return pl.pallas_call(
        main_kernel,
        in_specs=[SMEM] + whole(16) + [HBM] + whole(5),
        out_specs=whole(4),
        scratch_shapes=[
            pltpu.VMEM((NZ, NC, FB, 2 * width), jnp.bfloat16),
            pltpu.VMEM((2 * NZ, enc, FB), jnp.bfloat16),
            pltpu.VMEM((enc, 2 * width), jnp.float32),
            pltpu.VMEM((enc, 2 * width), jnp.bfloat16),
            pltpu.SemaphoreType.DMA((NZ, NC)),
        ],
        out_shape=[
            jax.ShapeDtypeStruct((dec, width), jnp.bfloat16),
            jax.ShapeDtypeStruct((enc, 2 * width), jnp.bfloat16),
            jax.ShapeDtypeStruct((4, NB, TB, FB), jnp.bfloat16),
            jax.ShapeDtypeStruct((4, NB, TB, FB), jnp.bfloat16),
        ],
        compiler_params=pltpu.CompilerParams(vmem_limit_bytes=28 << 20),
        name="main",
    )(place, *own, *other, weight, mark, query, grad, enc_col, dec_row)


def own_kernel(b, place_ref, grad_ref, w_ref, put):
    z, core, x, y = place_ref[0], place_ref[1], place_ref[2], place_ref[3]

    @pl.when(core == 0)
    def _():
        starts = [pl.multiple_of((NY * j + (y + b) % NY) * TB, TB) for j in range(NX)]
        grads = jnp.concatenate([grad_ref[pl.ds(start, TB), :] for start in starts], axis=0)
        for k in range(0, NZ, 2):
            rows = w_ref[pl.ds(k, 2), 0].reshape(2 * FB, grads.shape[1])
            out = lax.dot_general(grads, rows, NT, preferred_element_type=jnp.float32)
            for j in range(NX):
                for n in range(2):
                    put((j + NX - x) % NX, k + n, out[j * TB:(j + 1) * TB, n * FB:(n + 1) * FB])

    @pl.when(core == 1)
    def _():
        for i in range(0, 4, 2):
            rows = [w_ref[(z + Z_STEP[i + n] + 4 * b) % NZ, 1] for n in range(2)]
            out = lax.dot_general(grad_ref[...], jnp.concatenate(rows, axis=0), NT, preferred_element_type=jnp.float32)
            for n in range(2):
                put(i + n, slice(None), out[:, n * FB:(n + 1) * FB].reshape(NB, TB, FB))


def plain_kernel(b, place_ref, grad_ref, w_ref, out_ref):
    def put(i, k, value):
        out_ref[i, k] = value.astype(jnp.bfloat16)

    own_kernel(b, place_ref, grad_ref, w_ref, put)


def spread_own(b, place, grads, weight):
    return pl.pallas_call(
        functools.partial(plain_kernel, b),
        in_specs=[SMEM] + whole(2),
        out_specs=whole(1)[0],
        out_shape=jax.ShapeDtypeStruct((4, NB, TB, FB), jnp.bfloat16),
        compiler_params=pltpu.CompilerParams(vmem_limit_bytes=VMEM),
        name="spread_own",
    )(place, grads, weight)


def merge_kernel(one_ref, two_ref, *out_refs):
    for i in range(4):
        out_refs[i][...] = (one_ref[i].astype(jnp.float32) + two_ref[i].astype(jnp.float32)).astype(jnp.bfloat16)


def merge(one, two):
    shape = jax.ShapeDtypeStruct((NB, TB, FB), jnp.bfloat16)
    return pl.pallas_call(
        merge_kernel,
        in_specs=whole(2),
        out_specs=whole(4),
        out_shape=[shape] * 4,
        compiler_params=pltpu.CompilerParams(vmem_limit_bytes=VMEM),
        name="merge",
    )(one, two)


def total(parts):
    return functools.reduce(jnp.add, [p.astype(jnp.float32) for p in parts])


def per_device(enc_out, kv_weight, dec_query, ctx_grad, enc_seg, dec_seg):
    width = kv_weight.shape[3]
    place = jnp.stack([lax.axis_index(a) for a in AXES])

    near = small_stage(jnp.broadcast_to(enc_out, (NB, TB, FB)))
    far = across(near)
    own = [near] + [big_stage(near, i, -1) for i in (1, 2, 3)]
    own[1], far, kv_weight = lax.optimization_barrier((own[1], far, kv_weight))
    weight, mark = relayout(pltpu.with_memory_space_constraint(kv_weight, pltpu.HBM))
    held = pltpu.with_memory_space_constraint(weight, pltpu.HBM)
    own += [far] + [big_stage(far, i, -1) for i in (1, 2, 3)]
    *own[:5], mark = lax.optimization_barrier((*own[:5], mark))
    other = [pltpu.with_memory_space_constraint(twin(v), pltpu.HBM) for v in own]

    enc_col = enc_seg.reshape(NB * TB, 1)
    context, grads, home, away = main(place, own, other, held, mark, dec_query[0, 0], ctx_grad[0, 0], enc_col, dec_seg)
    away, home = twin(away), twin(home)
    away = merge(spread_own(1, place, grads, weight), away)
    *away, late = lax.optimization_barrier((*away, grads))
    away = [away[0]] + [big_stage(away[i], i, 1) for i in (1, 2, 3)]
    home = merge(spread_own(0, place, late, weight), home)
    home = [home[0]] + [big_stage(home[i], i, 1) for i in (1, 2, 3)]
    crossed = across(total(away).astype(jnp.bfloat16))
    planes = total(home + [crossed]).astype(jnp.bfloat16)
    owned = jnp.sum(small_stage(planes).astype(jnp.float32), axis=0)
    return context[None, None], owned[None]


def solution(mesh):
    fine = Mesh(mesh.devices.reshape(NZ, NC, NX, NY, ND), ("z", "c", "x", "y", "d"))
    section, mp = ("z", "c"), ("x", "y")
    placed = (
        P("d", mp, section),
        P(section, None, None, mp),
        P(section, "d", None, mp),
        P(section, "d", None, mp),
        P("d", None),
        P("d", None),
    )
    return jax.shard_map(
        per_device,
        mesh=fine,
        in_specs=placed,
        out_specs=(P(section, "d", None, mp), P("d", mp, section)),
        check_vma=False,
    )
```

```python
import functools

import jax
import jax.numpy as jnp
from jax import lax
from jax.experimental import pallas as pl
from jax.experimental.pallas import tpu as pltpu
from jax.sharding import Mesh, PartitionSpec as P

HD = 256
NZ, NC, NX, NY, ND = 8, 2, 4, 2, 2
TB = 64
FB = 256
NB = 8
VMEM = 20 << 20
AXES = ("z", "c", "x", "y")
NT = (((1,), (1,)), ((), ()))
TN = (((0,), (0,)), ((), ()))

Z_STEP = (0, 1, 2, 7)


def flat(z, c, x, y):
    return ((z * NC + c) * NX + x) * NY + y


SMALL_GROUPS = [[flat(z, 0, x, y) for z in range(NZ)] for x in range(NX) for y in range(NY)]
SMALL_GROUPS += [[flat(z, 1, x, y) for x in range(NX) for y in range(NY)] for z in range(NZ)]


def small_stage(value):
    return lax.all_to_all(value, AXES, 0, 0, axis_index_groups=SMALL_GROUPS)


def joint(value, move0, move1):
    pairs = []
    for z in range(NZ):
        for c in range(NC):
            for x in range(NX):
                for y in range(NY):
                    dz, dx, dy = (move0, move1)[c]
                    pairs.append((flat(z, c, x, y), flat((z + dz) % NZ, c, (x + dx) % NX, (y + dy) % NY)))
    return lax.ppermute(value, AXES, pairs)


def across(value):
    return joint(value, (0, 0, 1), (4, 0, 0))


def big_stage(value, i, sign):
    return joint(value, (0, sign * i, 0), (sign * Z_STEP[i], 0, 0))


def twin(value):
    return lax.ppermute(value, "c", [(0, 1), (1, 0)])


def whole(n):
    return [pl.BlockSpec(memory_space=pltpu.VMEM)] * n


HBM = pl.BlockSpec(memory_space=pltpu.HBM)
SMEM = pl.BlockSpec(memory_space=pltpu.SMEM)


def relayout_kernel(w_ref, out_ref, mark_ref, raw_ref, done_ref, load_sems, store_sems):
    def load(k):
        return pltpu.make_async_copy(w_ref.at[0, pl.ds(k * NC * FB, NC * FB)], raw_ref.at[k], load_sems.at[k])

    def store(k):
        return pltpu.make_async_copy(done_ref.at[k], out_ref.at[k], store_sems.at[k])

    for k in range(NZ):
        load(k).start()
    mark_ref[...] = jnp.zeros(mark_ref.shape, mark_ref.dtype)
    for k in range(NZ):
        load(k).wait()
        done_ref[k] = raw_ref[k].reshape(done_ref.shape[1:])
        store(k).start()
    for k in range(NZ):
        store(k).wait()


def relayout(weight):
    width = weight.shape[3]
    shape = (NZ, NC, FB, 2 * width)
    return pl.pallas_call(
        relayout_kernel,
        in_specs=[HBM],
        out_specs=[HBM] + whole(1),
        scratch_shapes=[
            pltpu.VMEM((NZ, NC * FB, 2, width), jnp.bfloat16),
            pltpu.VMEM(shape, jnp.bfloat16),
            pltpu.SemaphoreType.DMA((NZ,)),
            pltpu.SemaphoreType.DMA((NZ,)),
        ],
        out_shape=[pltpu.HBM(shape, jnp.bfloat16), jax.ShapeDtypeStruct((8, 128), jnp.float32)],
        compiler_params=pltpu.CompilerParams(vmem_limit_bytes=20 << 20),
        name="relayout",
    )(weight)


def lay_out(out_refs, parity, z, x, y, k, out):
    slot = (k + NZ - z) % NZ
    i = slot % 4
    b = (slot // 4 + i // 3) % 2
    for half in range(2):

        @pl.when((parity == 0) & (y == half))
        def _():
            for m in range(NB):
                out_refs[(m + half) % NY][(m // NY + NX - x) % NX, k] = out[m]

        @pl.when((parity == 1) & (b == half))
        def _():
            out_refs[half][i] = out


def load_weights(w_ref, w_buf, sems, k, core, slot):
    return pltpu.make_async_copy(w_ref.at[k, core], w_buf.at[k, slot], sems.at[k, slot])


def spread(grads, w_buf, slot, out_refs, parity, z, x, y):
    for k in range(0, NZ, 2):
        rows = w_buf[pl.ds(k, 2), slot].reshape(2 * FB, grads.shape[1])
        out = lax.dot_general(grads, rows, NT, preferred_element_type=jnp.float32).astype(jnp.bfloat16)
        for n in range(2):
            lay_out(out_refs, parity, z, x, y, k + n, out[:, n * FB:(n + 1) * FB].reshape(NB, TB, FB))


def attend(q, g, k, v, same):
    scale = HD ** -0.5
    scores = lax.dot_general(k, q, NT, preferred_element_type=jnp.float32) * scale
    scores = jnp.where(same, scores, -1e30)
    top = jnp.max(scores, axis=0, keepdims=True)
    raised = jnp.exp(scores - top)
    probs = raised / jnp.sum(raised, axis=0, keepdims=True)
    low = probs.astype(jnp.bfloat16)
    context = lax.dot_general(low, v, TN, preferred_element_type=jnp.float32).astype(jnp.bfloat16)
    grad_values = jnp.dot(low, g, preferred_element_type=jnp.float32).astype(jnp.bfloat16)
    gp = lax.dot_general(v, g, NT, preferred_element_type=jnp.float32)
    inner = jnp.sum(probs * gp, axis=0, keepdims=True)
    gs = (probs * (gp - inner) * scale).astype(jnp.bfloat16)
    grad_keys = jnp.dot(gs, q, preferred_element_type=jnp.float32).astype(jnp.bfloat16)
    return context, grad_keys, grad_values


def main_kernel(place_ref, *refs):
    own, other = refs[:8], refs[8:16]
    w_ref, _, q_ref, g_ref, es_ref, ds_ref, ctx_ref, grad_ref, home_ref, away_ref, w_buf, lhs_ref, acc_ref, kv_ref, sems = refs[16:]
    z, core, x, y = place_ref[0], place_ref[1], place_ref[2], place_ref[3]
    dec, width = q_ref.shape
    enc = NB * TB

    for k in range(NZ):
        for c in range(NC):
            load_weights(w_ref, w_buf, sems, k, c, c).start()

    def lay(even, odd):
        for b in range(2):
            for i in range(4):
                start = pl.multiple_of((((x + i) % NX) * NY + (y + b) % NY) * TB, TB)
                for k in range(NZ):
                    lhs_ref[2 * k, pl.ds(start, TB), :] = even[4 * b + i][k]
                lhs_ref[2 * ((z + Z_STEP[i] + 4 * b) % NZ) + 1] = odd[4 * b + i][...].reshape(enc, FB)

    @pl.when(core == 0)
    def _():
        lay(own, other)

    @pl.when(core == 1)
    def _():
        lay(other, own)

    for k in range(0, NZ, 2):
        for n in range(4):
            load_weights(w_ref, w_buf, sems, k + n // 2, n % 2, n % 2).wait()
        lhs = jnp.concatenate([lhs_ref[2 * k + n] for n in range(4)], axis=1)
        rows = w_buf[pl.ds(k, 2)].reshape(4 * FB, 2 * width)
        part = jnp.dot(lhs, rows, preferred_element_type=jnp.float32)
        if k == 0:
            acc_ref[...] = part
        elif k < NZ - 2:
            acc_ref[...] = acc_ref[...] + part
        else:
            kv_ref[...] = (acc_ref[...] + part).astype(jnp.bfloat16)

    same = es_ref[...] == ds_ref[...]
    for h in range(width // HD):
        head = pl.ds(h * HD, HD)
        value = pl.ds(width + h * HD, HD)
        found = attend(q_ref[:, head], g_ref[:, head], kv_ref[:, head], kv_ref[:, value], same)
        ctx_ref[:, head], grad_ref[:, head], grad_ref[:, value] = found

    spread(grad_ref[...], w_buf, 1 - core, (home_ref, away_ref), 1 - core, z, x, y)


def main(place, own, other, weight, mark, query, grad, enc_col, dec_row):
    dec, width = query.shape
    enc = NB * TB
    return pl.pallas_call(
        main_kernel,
        in_specs=[SMEM] + whole(16) + [HBM] + whole(5),
        out_specs=whole(4),
        scratch_shapes=[
            pltpu.VMEM((NZ, NC, FB, 2 * width), jnp.bfloat16),
            pltpu.VMEM((2 * NZ, enc, FB), jnp.bfloat16),
            pltpu.VMEM((enc, 2 * width), jnp.float32),
            pltpu.VMEM((enc, 2 * width), jnp.bfloat16),
            pltpu.SemaphoreType.DMA((NZ, NC)),
        ],
        out_shape=[
            jax.ShapeDtypeStruct((dec, width), jnp.bfloat16),
            jax.ShapeDtypeStruct((enc, 2 * width), jnp.bfloat16),
            jax.ShapeDtypeStruct((4, NB, TB, FB), jnp.bfloat16),
            jax.ShapeDtypeStruct((4, NB, TB, FB), jnp.bfloat16),
        ],
        compiler_params=pltpu.CompilerParams(vmem_limit_bytes=28 << 20),
        name="main",
    )(place, *own, *other, weight, mark, query, grad, enc_col, dec_row)


def own_kernel(b, place_ref, grad_ref, w_ref, put):
    z, core, x, y = place_ref[0], place_ref[1], place_ref[2], place_ref[3]

    @pl.when(core == 0)
    def _():
        starts = [pl.multiple_of((NY * j + (y + b) % NY) * TB, TB) for j in range(NX)]
        grads = jnp.concatenate([grad_ref[pl.ds(start, TB), :] for start in starts], axis=0)
        for k in range(0, NZ, 2):
            rows = w_ref[pl.ds(k, 2), 0].reshape(2 * FB, grads.shape[1])
            out = lax.dot_general(grads, rows, NT, preferred_element_type=jnp.float32)
            for j in range(NX):
                for n in range(2):
                    put((j + NX - x) % NX, k + n, out[j * TB:(j + 1) * TB, n * FB:(n + 1) * FB])

    @pl.when(core == 1)
    def _():
        for i in range(0, 4, 2):
            rows = [w_ref[(z + Z_STEP[i + n] + 4 * b) % NZ, 1] for n in range(2)]
            out = lax.dot_general(grad_ref[...], jnp.concatenate(rows, axis=0), NT, preferred_element_type=jnp.float32)
            for n in range(2):
                put(i + n, slice(None), out[:, n * FB:(n + 1) * FB].reshape(NB, TB, FB))


def plain_kernel(b, place_ref, grad_ref, w_ref, out_ref):
    def put(i, k, value):
        out_ref[i, k] = value.astype(jnp.bfloat16)

    own_kernel(b, place_ref, grad_ref, w_ref, put)


def spread_own(b, place, grads, weight):
    return pl.pallas_call(
        functools.partial(plain_kernel, b),
        in_specs=[SMEM] + whole(2),
        out_specs=whole(1)[0],
        out_shape=jax.ShapeDtypeStruct((4, NB, TB, FB), jnp.bfloat16),
        compiler_params=pltpu.CompilerParams(vmem_limit_bytes=VMEM),
        name="spread_own",
    )(place, grads, weight)


def merge_kernel(one_ref, two_ref, *out_refs):
    for i in range(4):
        out_refs[i][...] = (one_ref[i].astype(jnp.float32) + two_ref[i].astype(jnp.float32)).astype(jnp.bfloat16)


def merge(one, two):
    shape = jax.ShapeDtypeStruct((NB, TB, FB), jnp.bfloat16)
    return pl.pallas_call(
        merge_kernel,
        in_specs=whole(2),
        out_specs=whole(4),
        out_shape=[shape] * 4,
        compiler_params=pltpu.CompilerParams(vmem_limit_bytes=VMEM),
        name="merge",
    )(one, two)


def total(parts):
    return functools.reduce(jnp.add, [p.astype(jnp.float32) for p in parts])


def per_device(enc_out, kv_weight, dec_query, ctx_grad, enc_seg, dec_seg):
    width = kv_weight.shape[3]
    place = jnp.stack([lax.axis_index(a) for a in AXES])

    near = small_stage(jnp.broadcast_to(enc_out, (NB, TB, FB)))
    far = across(near)
    own = [near] + [big_stage(near, i, -1) for i in (1, 2, 3)]
    first = twin(near)
    first, own[1], far, kv_weight = lax.optimization_barrier((first, own[1], far, kv_weight))
    weight, mark = relayout(pltpu.with_memory_space_constraint(kv_weight, pltpu.HBM))
    held = pltpu.with_memory_space_constraint(weight, pltpu.HBM)
    own += [far] + [big_stage(far, i, -1) for i in (1, 2, 3)]
    *own[1:5], mark = lax.optimization_barrier((*own[1:5], mark))
    other = [pltpu.with_memory_space_constraint(v, pltpu.HBM) for v in [first] + [twin(v) for v in own[1:]]]

    enc_col = enc_seg.reshape(NB * TB, 1)
    context, grads, home, away = main(place, own, other, held, mark, dec_query[0, 0], ctx_grad[0, 0], enc_col, dec_seg)
    away, home = twin(away), twin(home)
    away = merge(spread_own(1, place, grads, weight), away)
    *away, late = lax.optimization_barrier((*away, grads))
    away = [away[0]] + [big_stage(away[i], i, 1) for i in (1, 2, 3)]
    home = merge(spread_own(0, place, late, weight), home)
    home = [home[0]] + [big_stage(home[i], i, 1) for i in (1, 2, 3)]
    crossed = across(total(away).astype(jnp.bfloat16))
    planes = total(home + [crossed]).astype(jnp.bfloat16)
    owned = jnp.sum(small_stage(planes).astype(jnp.float32), axis=0)
    return context[None, None], owned[None]


def solution(mesh):
    fine = Mesh(mesh.devices.reshape(NZ, NC, NX, NY, ND), ("z", "c", "x", "y", "d"))
    section, mp = ("z", "c"), ("x", "y")
    placed = (
        P("d", mp, section),
        P(section, None, None, mp),
        P(section, "d", None, mp),
        P(section, "d", None, mp),
        P("d", None),
        P("d", None),
    )
    return jax.shard_map(
        per_device,
        mesh=fine,
        in_specs=placed,
        out_specs=(P(section, "d", None, mp), P("d", mp, section)),
        check_vma=False,
    )
```
